256 devices in a mesh: tm: 8 (over z), lat: 4 (over x), lon: 8 (over y, core).
Axes of the slice: x: 4, y: 4, z: 8, core: 2. Of those that a mesh axis runs over, the one named last changes fastest.
Arguments:
- slab: bfloat16 [512, 262144], P('tm', ('lat', 'lon')), may hold values from -6 to 6
- start: bfloat16 [512, 64], P('tm'), may hold values from -6 to 6
- sections: float32 [3, 2], replicated, may hold values from 0.2 to 1.5708, as said below
Outputs:
- basis: float32 [2048, 64, 128], P(('lat', 'lon', 'tm'))
- pcs: float32 [512, 64], P('tm')
The draws below stay inside these ranges and needn't reach their ends.
Inputs may be any that keep to these rules, and one draw needn't show every extreme that they name: `sections`: in each column, one section has radius 0.78 to 0.86 and angle 2 pi / 8 to 2 pi / 4, the other radius 0.9955 to 0.9985 and angle 2 pi / 24 to 2 pi / 12; which column is which varies; amplitudes 0.2 to 1.0.
All inputs are finite; a program needn't handle non-finite values.
Results may differ from the reference program's by a relative error of at most 0.0039.
Values may be sent and summed in bfloat16 or wider, within the bound.
A program may use at most 64 MiB of HBM per device.

```python
import math
import jax
import jax.numpy as jnp
from jax import lax

HOURS = 512
K = 64
LANES = 128
CELLS = 262144
GROUPS = 2048


def draw_sections(key, part):
    picks = jax.random.uniform(key, (3, 2), jnp.float32)
    broad = jnp.stack([0.78 + 0.08 * picks[0, 0], 2.0 * math.pi / (4.0 + 4.0 * picks[1, 0]), 0.6 + 0.4 * picks[2, 0]])
    slower = jnp.stack([0.9955 + 0.003 * picks[0, 1], 2.0 * math.pi / (12.0 + 12.0 * picks[1, 1]), 0.2 + 0.15 * picks[2, 1]])
    flipped = jax.random.randint(jax.random.fold_in(key, 7), (), 0, 2)
    first_column = jnp.where(flipped == 0, broad, slower)
    second_column = jnp.where(flipped == 0, slower, broad)
    return jnp.stack([first_column, second_column], axis=1).astype(jnp.float32)


def shard_levels(key, dims, split, low, top_value):
    gain, own = 1.0, jax.random.fold_in(key, 6)
    for position, shards_of in split:
        heights = jnp.exp(jax.random.uniform(jax.random.fold_in(own, position), (shards_of,), jnp.float32, low / len(split), top_value / len(split)))
        gain = gain * jnp.repeat(heights, dims[position] // shards_of).reshape([-1 if axis == position else 1 for axis in range(len(dims))])
    return gain


def gaussian(rng, shape, deviation, most, split=(), held_as=jnp.bfloat16):
    values = deviation * jax.random.normal(rng, shape, jnp.float32)
    if split:
        values = values * shard_levels(rng, shape, split, -0.22, 0.18)
    return jnp.clip(values, -most, most).astype(held_as)


def setup_inputs(seed: int = 0) -> dict:
    key_of = jax.random.split(jax.random.key(seed), 4)
    slab = gaussian(key_of[0], (HOURS, CELLS), 1.0, 6.0, ((0, 8), (1, 32)))
    start = gaussian(key_of[1], (HOURS, K), 1.0, 6.0, ((0, 8),))
    sections = draw_sections(jax.random.fold_in(key_of[3], 71), 0)
    return {"slab": slab, "start": start, "sections": sections}


def filter_rows(sections):
    radius = sections[0]
    angles = sections[1]
    amplitude = sections[2]
    feed_one = 2.0 * radius * jnp.cos(angles)
    feed_two = -radius * radius
    drive_gain = amplitude * jnp.sqrt(1.0 - radius * radius)
    return (feed_one, feed_two, drive_gain)

def advance(carried, inputs, coefficients):
    feed_one, feed_two, drive_gain = coefficients
    residual_gap = inputs - carried[1]
    section_one = drive_gain[0] * residual_gap + feed_one[0] * carried[2] + feed_two[0] * carried[3]
    section_two = drive_gain[1] * residual_gap + feed_one[1] * carried[4] + feed_two[1] * carried[5]
    updated = jnp.stack([inputs, carried[0], section_one, carried[2], section_two, carried[4]])
    return (updated, section_one + section_two)

def reference(slab, start, sections):
    coefficients = filter_rows(sections)
    cell_count = slab.shape[1]

    def hour_step(carried, row_values):
        updated, output = advance(carried, row_values.astype(jnp.float32), coefficients)
        return (updated, output.astype(jnp.bfloat16))
    initial = jnp.zeros((6, cell_count), jnp.float32)
    _, filtered = lax.scan(hour_step, initial, slab)
    spatial_patterns = jnp.dot(start.T.astype(jnp.float32), filtered.astype(jnp.float32), preferred_element_type=jnp.float32)
    gram_matrix = jnp.dot(spatial_patterns, spatial_patterns.T, precision=lax.Precision.HIGHEST)
    lower_factor = jnp.linalg.cholesky(gram_matrix)
    inverse_factor = jax.scipy.linalg.solve_triangular(lower_factor, jnp.eye(K, dtype=jnp.float32), lower=True)
    ortho = jnp.dot(inverse_factor, spatial_patterns, precision=lax.Precision.HIGHEST)
    basis = (ortho * math.sqrt(CELLS)).reshape(K, GROUPS, LANES).transpose(1, 0, 2)

    def project_block(block_of_rows):
        return jnp.dot(block_of_rows.astype(jnp.float32), ortho.T, precision=lax.Precision.HIGHEST)
    blocks = filtered.reshape(8, HOURS // 8, CELLS)
    pcs = lax.map(project_block, blocks).reshape(HOURS, K) * math.sqrt(HOURS / CELLS)
    return (basis, pcs)
```

```python
import functools
import math

import jax
import jax.numpy as jnp
from jax import lax
from jax.experimental import pallas as pl
from jax.experimental.pallas import tpu as pltpu
from jax.sharding import PartitionSpec as P

LANES = 128
BLOCK = 128
CHUNKS = 4
MESH = pl.DeviceIdType.MESH
FULL = lax.Precision.HIGHEST


def lane_rows(shape, axis):
    return lax.broadcasted_iota(jnp.int32, shape, axis)


def toeplitz_blocks(sections_ref, count):
    shape = (BLOCK, BLOCK)
    offset = lane_rows(shape, 0) - lane_rows(shape, 1)
    moment = offset.astype(jnp.float32)
    totals = [jnp.zeros(shape, jnp.float32) for _ in range(count)]
    at_zero = jnp.zeros((8, LANES), jnp.float32)
    for section in range(2):
        radius = jnp.full((8, LANES), sections_ref[0, section], jnp.float32)
        angle = jnp.full((8, LANES), sections_ref[1, section], jnp.float32)
        amplitude = jnp.full((8, LANES), sections_ref[2, section], jnp.float32)
        drive = amplitude * jnp.sqrt(1.0 - radius * radius)
        at_zero = at_zero + drive
        back = 1.0 / (radius * radius)
        sine, cosine = jnp.sin(angle), jnp.cos(angle)
        sine_part = drive * (1.0 - back) * cosine / sine
        cosine_part = drive * (1.0 + back)
        log_radius = jnp.log(radius)
        size = jnp.exp(moment * log_radius[:1])
        turn = moment * angle[:1]
        sine_of, cosine_of = size * jnp.sin(turn), size * jnp.cos(turn)
        for block in range(count):
            far = float(block * BLOCK)
            gain = jnp.exp(far * log_radius)
            far_sine, far_cosine = jnp.sin(far * angle), jnp.cos(far * angle)
            on_sine = gain * (sine_part * far_cosine - cosine_part * far_sine)
            on_cosine = gain * (sine_part * far_sine + cosine_part * far_cosine)
            totals[block] = totals[block] + on_sine[:1] * sine_of + on_cosine[:1] * cosine_of
    first = jnp.where(offset > 0, totals[0], jnp.where(offset == 0, at_zero[:1], 0.0))
    return [first] + totals[1:]


def factor_inverse(gram):
    width = gram.shape[0]
    count = width // 8
    rows = [gram[8 * m : 8 * m + 8] for m in range(count)]
    sub = lane_rows((8, LANES), 0)

    def spread(value, row):
        return jnp.broadcast_to(value[row : row + 1], (8, LANES))

    def step(position, rows):
        rows = list(rows)
        live = [(m < count - position).astype(jnp.float32) for m in range(count)]
        columns = [
            [jnp.broadcast_to(rows[m][:, j : j + 1], (8, LANES)) for m in range(count)] for j in range(8)
        ]
        head = rows[0]
        scale = jnp.ones((8, LANES), jnp.float32)
        scaled_rows = []
        for j in range(8):
            pivot = spread(columns[j][0], j)
            inverse_pivot = 1.0 / pivot
            scale = jnp.where(sub == j, lax.rsqrt(pivot), scale)
            columns[j][0] = jnp.where(sub > j, columns[j][0], 0.0)
            for k in range(j + 1, 8):
                weight = spread(columns[k][0], j) * inverse_pivot
                columns[k] = [ck - cj * weight for ck, cj in zip(columns[k], columns[j])]
            scaled = spread(head, j) * inverse_pivot
            scaled_rows.append(scaled)
            head = head - columns[j][0] * scaled
        out = []
        for m in range(1, count):
            taken = columns[0][m] * scaled_rows[0]
            for j in range(1, 8):
                taken = taken + columns[j][m] * scaled_rows[j]
            out.append(rows[m] - live[m] * taken)
        out.append(head * scale)
        return tuple(pltpu.roll(value, 2 * width - 8, 1) for value in out)

    rows = lax.fori_loop(0, count, step, tuple(rows))
    return jnp.concatenate(rows, axis=0)


def kernel(
    sizes,
    slab_ref, start_ref, sections_ref,
    basis_ref, pcs_ref,
    cells_ref, starts_ref, high_ref, low_ref, patterns_ref,
    gram_ref, gram_tm_ref, gram_xy_ref, gram_all_ref,
    shares_ref, shares_tm_ref, shares_xy_ref,
    local_sem, cells_send, cells_recv, starts_send, starts_recv,
    gram_send, gram_recv, shares_send, shares_recv,
    far_gram_send, far_gram_recv, far_shares_send, far_shares_recv,
    all_send, all_recv,
):
    tm_count, lat_count, lon_count, hour_count, width, own_cells = sizes
    hours_all = tm_count * hour_count
    chunk = own_cells // CHUNKS
    plane = lat_count * lon_count
    cells_all = own_cells * tm_count * plane
    tm, lat, lon = lax.axis_index("tm"), lax.axis_index("lat"), lax.axis_index("lon")
    here = lat * lon_count + lon
    order = sorted(range(1, tm_count), key=lambda d: -min(d, tm_count - d))

    barrier = pltpu.get_barrier_semaphore()

    def tm_peer(distance):
        return lax.rem(tm + distance, tm_count)

    def plane_peer(offset):
        other = lax.rem(lat + offset // lon_count, lat_count), lax.rem(lon + lax.rem(offset, lon_count), lon_count)
        return {"lat": other[0], "lon": other[1]}, other[0] * lon_count + other[1]

    for distance in order:
        pl.semaphore_signal(barrier, inc=1, device_id={"tm": tm_peer(distance)}, device_id_type=MESH)

    def greet(offset, carry):
        pl.semaphore_signal(barrier, inc=1, device_id=plane_peer(offset)[0], device_id_type=MESH)
        return carry

    lax.fori_loop(1, plane, greet, 0)

    def hours_of(index):
        return pl.ds(pl.multiple_of(index * hour_count, hour_count), hour_count)

    def cells_of(index, part):
        return pl.ds(pl.multiple_of(index * own_cells + part * chunk, chunk), chunk)

    own = [
        pltpu.make_async_copy(slab_ref.at[:, cells_of(tm, part)], cells_ref.at[part, hours_of(tm)], local_sem.at[part])
        for part in range(CHUNKS)
    ]
    own_start = pltpu.make_async_copy(start_ref, starts_ref.at[hours_of(tm)], local_sem.at[CHUNKS])
    for copy in own:
        copy.start()
    own_start.start()

    def send_cells(distance, part, index):
        return pltpu.make_async_remote_copy(
            src_ref=slab_ref.at[:, cells_of(index, part)],
            dst_ref=cells_ref.at[part, hours_of(tm)],
            send_sem=cells_send.at[part, distance],
            recv_sem=cells_recv.at[part, tm],
            device_id={"tm": index},
            device_id_type=MESH,
        )

    def take_cells(part, index):
        return pltpu.make_async_remote_copy(
            src_ref=slab_ref.at[:, cells_of(tm, part)],
            dst_ref=cells_ref.at[part, hours_of(index)],
            send_sem=cells_send.at[part, 0],
            recv_sem=cells_recv.at[part, index],
            device_id={"tm": index},
            device_id_type=MESH,
        )

    def send_start(distance, index, slot):
        return pltpu.make_async_remote_copy(
            src_ref=start_ref,
            dst_ref=starts_ref.at[hours_of(slot)],
            send_sem=starts_send.at[distance],
            recv_sem=starts_recv.at[slot],
            device_id={"tm": index},
            device_id_type=MESH,
        )

    pl.semaphore_wait(barrier, tm_count - 1 + plane - 1)

    for part in range(CHUNKS):
        for distance in order:
            send_cells(distance, part, tm_peer(distance)).start()
        if part == 0:
            for distance in order:
                send_start(distance, tm_peer(distance), tm).start()

    high_ref[...] = jnp.zeros_like(high_ref)
    low_ref[...] = jnp.zeros_like(low_ref)
    block_count = hours_all // BLOCK
    for lag, values in enumerate(toeplitz_blocks(sections_ref, block_count)):
        top = values.astype(jnp.bfloat16)
        rest = (values - top.astype(jnp.float32)).astype(jnp.bfloat16)
        for column in range(block_count - lag):
            place = (pl.ds((column + lag) * BLOCK, BLOCK), pl.ds(column * BLOCK, BLOCK))
            high_ref[place] = top
            low_ref[place] = rest

    own_start.wait()
    for distance in order:
        send_start(distance, tm_peer(distance), tm_peer(distance)).wait_recv()
    starts = starts_ref[...]

    gram_total = jnp.zeros((2 * width, 2 * width), jnp.float32)
    shares_total = jnp.zeros((hours_all, 2 * width), jnp.float32)
    half = hours_all // 2
    for part in range(CHUNKS):
        own[part].wait()
        for distance in order:
            take_cells(part, tm_peer(distance)).wait_recv()
        upper = [
            jnp.dot(ref[:half, :half], cells_ref[part, :half], preferred_element_type=jnp.float32)
            for ref in (high_ref, low_ref)
        ]
        lower = [
            jnp.dot(ref[half:], cells_ref[part], preferred_element_type=jnp.float32) for ref in (high_ref, low_ref)
        ]
        filtered = jnp.concatenate([upper[0] + upper[1], lower[0] + lower[1]], axis=0).astype(jnp.bfloat16)
        patterns = lax.dot_general(starts, filtered, (((0,), (0,)), ((), ())), preferred_element_type=jnp.float32)
        patterns_ref[:, part * chunk : (part + 1) * chunk] = patterns
        top = patterns.astype(jnp.bfloat16)
        rest = (patterns - top.astype(jnp.float32)).astype(jnp.bfloat16)
        both = jnp.concatenate([top, rest], axis=0)
        by_rows = (((1,), (1,)), ((), ()))
        gram_total = gram_total + lax.dot_general(both, both, by_rows, preferred_element_type=jnp.float32)
        shares_total = shares_total + lax.dot_general(filtered, both, by_rows, preferred_element_type=jnp.float32)

    def folded(value):
        return value + pltpu.roll(value, width, 1)

    gram_here = folded(gram_total[:width] + gram_total[width:])
    rows_each = width // tm_count
    for index in range(tm_count):
        gram_ref[index] = gram_here[index * rows_each : (index + 1) * rows_each]

    def send_gram(distance, index, slot):
        return pltpu.make_async_remote_copy(
            src_ref=gram_ref.at[index],
            dst_ref=gram_tm_ref.at[slot],
            send_sem=gram_send.at[distance],
            recv_sem=gram_recv.at[slot],
            device_id={"tm": index},
            device_id_type=MESH,
        )

    def send_shares(distance, index, slot):
        return pltpu.make_async_remote_copy(
            src_ref=shares_ref.at[index],
            dst_ref=shares_tm_ref.at[slot],
            send_sem=shares_send.at[distance],
            recv_sem=shares_recv.at[slot],
            device_id={"tm": index},
            device_id_type=MESH,
        )

    for distance in order:
        send_gram(distance, tm_peer(distance), tm).start()

    shares_here = folded(shares_total)
    left = lane_rows((hour_count // 2, 2 * width), 1) < width
    for index in range(tm_count):
        base = index * hour_count
        middle = base + hour_count // 2
        shares_ref[index] = jnp.where(left, shares_here[base:middle], shares_here[middle : base + hour_count])
    for distance in order:
        send_shares(distance, tm_peer(distance), tm).start()

    gram_tm_ref[tm] = gram_ref[tm]
    for distance in order:
        send_gram(distance, tm_peer(distance), tm_peer(distance)).wait_recv()
    gram_xy_ref[here] = jnp.sum(gram_tm_ref[...], axis=0)

    def send_far(source, slots, sends, receives, offset, slot):
        return pltpu.make_async_remote_copy(
            src_ref=source.at[here],
            dst_ref=slots.at[slot],
            send_sem=sends.at[offset],
            recv_sem=receives.at[slot],
            device_id=plane_peer(offset)[0],
            device_id_type=MESH,
        )

    far_gram = functools.partial(send_far, gram_xy_ref, gram_xy_ref, far_gram_send, far_gram_recv)
    far_shares = functools.partial(send_far, shares_xy_ref, shares_xy_ref, far_shares_send, far_shares_recv)

    def over_plane(action):
        def step(offset, carry):
            action(offset)
            return carry

        lax.fori_loop(1, plane, step, 0)

    over_plane(lambda offset: far_gram(offset, here).start())

    shares_tm_ref[tm] = shares_ref[tm]
    for distance in order:
        send_shares(distance, tm_peer(distance), tm_peer(distance)).wait_recv()
    shares_xy_ref[here] = jnp.sum(shares_tm_ref[...], axis=0)
    over_plane(lambda offset: far_shares(offset, here).start())

    over_plane(lambda offset: far_gram(offset, plane_peer(offset)[1]).wait_recv())
    gram_all_ref[tm] = jnp.sum(gram_xy_ref[...], axis=0)

    def send_all(distance, index, slot):
        return pltpu.make_async_remote_copy(
            src_ref=gram_all_ref.at[tm],
            dst_ref=gram_all_ref.at[slot],
            send_sem=all_send.at[distance],
            recv_sem=all_recv.at[slot],
            device_id={"tm": index},
            device_id_type=MESH,
        )

    for distance in order:
        send_all(distance, tm_peer(distance), tm).start()
    for distance in order:
        send_all(distance, tm_peer(distance), tm_peer(distance)).wait_recv()

    gram = gram_all_ref[...].reshape(width, 2 * width)
    shape = (width, 2 * width)
    unit = jnp.where(lane_rows(shape, 1) - width == lane_rows(shape, 0), 1.0, 0.0)
    inverse = factor_inverse(jnp.where(lane_rows(shape, 1) < width, gram, unit))[:, :width]

    scaled = inverse * math.sqrt(cells_all)
    ortho = jnp.dot(scaled, patterns_ref[...], preferred_element_type=jnp.float32, precision=FULL)
    for group in range(own_cells // LANES):
        basis_ref[group] = ortho[:, group * LANES : (group + 1) * LANES]

    over_plane(lambda offset: far_shares(offset, plane_peer(offset)[1]).wait_recv())
    packed = jnp.sum(shares_xy_ref[...], axis=0)
    shares = jnp.concatenate([packed, pltpu.roll(packed, width, 1)], axis=0)[:, :width]
    pcs_ref[...] = lax.dot_general(
        shares, inverse * math.sqrt(hours_all / cells_all), (((1,), (1,)), ((), ())),
        preferred_element_type=jnp.float32, precision=FULL,
    )

    for distance in order:
        for part in range(CHUNKS):
            send_cells(distance, part, tm_peer(distance)).wait_send()
        send_start(distance, tm_peer(distance), tm).wait_send()
        send_gram(distance, tm_peer(distance), tm).wait_send()
        send_shares(distance, tm_peer(distance), tm).wait_send()
        send_all(distance, tm_peer(distance), tm).wait_send()
    over_plane(lambda offset: far_gram(offset, here).wait_send())
    over_plane(lambda offset: far_shares(offset, here).wait_send())


def solution(mesh):
    tm_count, lat_count, lon_count = mesh.shape["tm"], mesh.shape["lat"], mesh.shape["lon"]
    plane = lat_count * lon_count

    def local(slab, start, sections):
        hour_count, cell_count = slab.shape
        width = start.shape[1]
        own_cells = cell_count // tm_count
        hours_all = hour_count * tm_count
        chunk = own_cells // CHUNKS
        rows_each = width // tm_count
        sizes = (tm_count, lat_count, lon_count, hour_count, width, own_cells)
        dma = pltpu.SemaphoreType.DMA
        f32, bf16 = jnp.float32, jnp.bfloat16
        return pl.pallas_call(
            functools.partial(kernel, sizes),
            out_shape=(
                jax.ShapeDtypeStruct((own_cells // LANES, width, LANES), f32),
                jax.ShapeDtypeStruct((hour_count, width), f32),
            ),
            in_specs=[
                pl.BlockSpec(memory_space=pl.ANY),
                pl.BlockSpec(memory_space=pl.ANY),
                pl.BlockSpec(memory_space=pltpu.SMEM),
            ],
            out_specs=(pl.BlockSpec(memory_space=pltpu.VMEM), pl.BlockSpec(memory_space=pltpu.VMEM)),
            scratch_shapes=[
                pltpu.VMEM((CHUNKS, hours_all, chunk), bf16),
                pltpu.VMEM((hours_all, width), bf16),
                pltpu.VMEM((hours_all, hours_all), bf16),
                pltpu.VMEM((hours_all, hours_all), bf16),
                pltpu.VMEM((width, own_cells), f32),
                pltpu.VMEM((tm_count, rows_each, 2 * width), f32),
                pltpu.VMEM((tm_count, rows_each, 2 * width), f32),
                pltpu.VMEM((plane, rows_each, 2 * width), f32),
                pltpu.VMEM((tm_count, rows_each, 2 * width), f32),
                pltpu.VMEM((tm_count, hour_count // 2, 2 * width), f32),
                pltpu.VMEM((tm_count, hour_count // 2, 2 * width), f32),
                pltpu.VMEM((plane, hour_count // 2, 2 * width), f32),
                dma((CHUNKS + 1,)),
                dma((CHUNKS, tm_count)), dma((CHUNKS, tm_count)),
                dma((tm_count,)), dma((tm_count,)),
                dma((tm_count,)), dma((tm_count,)),
                dma((tm_count,)), dma((tm_count,)),
                dma((plane,)), dma((plane,)),
                dma((plane,)), dma((plane,)),
                dma((tm_count,)), dma((tm_count,)),
            ],
            compiler_params=pltpu.CompilerParams(
                collective_id=0, has_side_effects=True, vmem_limit_bytes=48 * 1024 * 1024
            ),
        )(slab, start, sections)

    return jax.shard_map(
        local,
        mesh=mesh,
        in_specs=(P("tm", ("lat", "lon")), P("tm", None), P()),
        out_specs=(P(("lat", "lon", "tm"), None, None), P("tm", None)),
        check_vma=False,
    )
```

```python
import functools
import math

import jax
import jax.numpy as jnp
from jax import lax
from jax.experimental import pallas as pl
from jax.experimental.pallas import tpu as pltpu
from jax.sharding import PartitionSpec as P

LANES = 128
BLOCK = 128
CHUNKS = 4
MESH = pl.DeviceIdType.MESH
FULL = lax.Precision.HIGHEST


def lane_rows(shape, axis):
    return lax.broadcasted_iota(jnp.int32, shape, axis)


def toeplitz_blocks(sections_ref, count):
    shape = (BLOCK, BLOCK)
    offset = lane_rows(shape, 0) - lane_rows(shape, 1)
    moment = offset.astype(jnp.float32)
    totals = [jnp.zeros(shape, jnp.float32) for _ in range(count)]
    at_zero = jnp.zeros((8, LANES), jnp.float32)
    for section in range(2):
        radius = jnp.full((8, LANES), sections_ref[section, 0], jnp.float32)
        angle = jnp.full((8, LANES), sections_ref[section, 1], jnp.float32)
        amplitude = jnp.full((8, LANES), sections_ref[section, 2], jnp.float32)
        drive = amplitude * jnp.sqrt(1.0 - radius * radius)
        at_zero = at_zero + drive
        back = 1.0 / (radius * radius)
        sine, cosine = jnp.sin(angle), jnp.cos(angle)
        sine_part = drive * (1.0 - back) * cosine / sine
        cosine_part = drive * (1.0 + back)
        log_radius = jnp.log(radius)
        size = jnp.exp(moment * log_radius[:1])
        turn = moment * angle[:1]
        sine_of, cosine_of = size * jnp.sin(turn), size * jnp.cos(turn)
        for block in range(count):
            far = float(block * BLOCK)
            gain = jnp.exp(far * log_radius)
            far_sine, far_cosine = jnp.sin(far * angle), jnp.cos(far * angle)
            on_sine = gain * (sine_part * far_cosine - cosine_part * far_sine)
            on_cosine = gain * (sine_part * far_sine + cosine_part * far_cosine)
            totals[block] = totals[block] + on_sine[:1] * sine_of + on_cosine[:1] * cosine_of
    first = jnp.where(offset > 0, totals[0], jnp.where(offset == 0, at_zero[:1], 0.0))
    return [first] + totals[1:]


def factor_inverse(gram):
    width = gram.shape[0]
    count = width // 8
    rows = [gram[8 * m : 8 * m + 8] for m in range(count)]
    sub = lane_rows((8, LANES), 0)

    def spread(value, row):
        return jnp.broadcast_to(value[row : row + 1], (8, LANES))

    def step(position, rows):
        rows = list(rows)
        live = [(m < count - position).astype(jnp.float32) for m in range(count)]
        columns = [
            [jnp.broadcast_to(rows[m][:, j : j + 1], (8, LANES)) for m in range(count)] for j in range(8)
        ]
        head = rows[0]
        scale = jnp.ones((8, LANES), jnp.float32)
        scaled_rows = []
        for j in range(8):
            pivot = spread(columns[j][0], j)
            inverse_pivot = 1.0 / pivot
            scale = jnp.where(sub == j, lax.rsqrt(pivot), scale)
            columns[j][0] = jnp.where(sub > j, columns[j][0], 0.0)
            for k in range(j + 1, 8):
                weight = spread(columns[k][0], j) * inverse_pivot
                columns[k] = [ck - cj * weight for ck, cj in zip(columns[k], columns[j])]
            scaled = spread(head, j) * inverse_pivot
            scaled_rows.append(scaled)
            head = head - columns[j][0] * scaled
        out = []
        for m in range(1, count):
            taken = columns[0][m] * scaled_rows[0]
            for j in range(1, 8):
                taken = taken + columns[j][m] * scaled_rows[j]
            out.append(rows[m] - live[m] * taken)
        out.append(head * scale)
        return tuple(pltpu.roll(value, 2 * width - 8, 1) for value in out)

    rows = lax.fori_loop(0, count, step, tuple(rows))
    return jnp.concatenate(rows, axis=0)


def kernel(
    sizes,
    slab_in, start_in, sections_in,
    basis_ref, pcs_ref,
    slab_ref, start_ref, sections_ref,
    cells_ref, starts_ref, high_ref, low_ref, patterns_ref,
    gram_ref, gram_lon_ref, gram_lat_ref, gram_tm_ref, gram_all_ref,
    shares_ref, shares_tm_ref, shares_lat_ref, shares_lon_ref,
    local_sem, cells_send, cells_recv, starts_send, starts_recv,
    *stage_sems,
):
    tm_count, lat_count, lon_count, hour_count, width, own_cells = sizes
    hours_all = tm_count * hour_count
    chunk = own_cells // CHUNKS
    cells_all = own_cells * tm_count * lat_count * lon_count
    counts = {"tm": tm_count, "lat": lat_count, "lon": lon_count}
    place = {axis: lax.axis_index(axis) for axis in counts}
    tm, lat, lon = place["tm"], place["lat"], place["lon"]

    loads = [
        pltpu.make_async_copy(sections_in, sections_ref, local_sem.at[0]),
        pltpu.make_async_copy(slab_in, slab_ref, local_sem.at[1]),
        pltpu.make_async_copy(start_in, start_ref, local_sem.at[2]),
    ]
    for copy in loads:
        copy.start()

    def peer(axis, distance):
        return lax.rem(place[axis] + distance, counts[axis])

    def far_first(axis):
        count = counts[axis]
        return sorted(range(1, count), key=lambda d: -min(d, count - d))

    order = far_first("tm")
    barrier = pltpu.get_barrier_semaphore()
    for axis in ("tm", "lon", "lat"):
        for distance in far_first(axis):
            pl.semaphore_signal(barrier, inc=1, device_id={axis: peer(axis, distance)}, device_id_type=MESH)

    def hours_of(index):
        return pl.ds(pl.multiple_of(index * hour_count, hour_count), hour_count)

    def cells_of(index, part):
        return pl.ds(pl.multiple_of(index * own_cells + part * chunk, chunk), chunk)

    def send_cells(part, distance, index, slot):
        return pltpu.make_async_remote_copy(
            src_ref=slab_ref.at[:, cells_of(index, part)],
            dst_ref=cells_ref.at[part, hours_of(slot)],
            send_sem=cells_send.at[part, distance],
            recv_sem=cells_recv.at[part, slot],
            device_id={"tm": index},
            device_id_type=MESH,
        )

    def send_start(distance, index, slot):
        return pltpu.make_async_remote_copy(
            src_ref=start_ref,
            dst_ref=starts_ref.at[hours_of(slot)],
            send_sem=starts_send.at[distance],
            recv_sem=starts_recv.at[slot],
            device_id={"tm": index},
            device_id_type=MESH,
        )

    class Stage:
        def __init__(self, number, axis, source, slots):
            self.axis, self.source, self.slots = axis, source, slots
            self.sends, self.receives = stage_sems[2 * number], stage_sems[2 * number + 1]

        def copy(self, distance, slot):
            index = peer(self.axis, distance)
            return pltpu.make_async_remote_copy(
                src_ref=self.source(index),
                dst_ref=self.slots.at[slot],
                send_sem=self.sends.at[distance],
                recv_sem=self.receives.at[slot],
                device_id={self.axis: index},
                device_id_type=MESH,
            )

        def start(self):
            for distance in far_first(self.axis):
                self.copy(distance, place[self.axis]).start()

        def receive(self):
            for distance in reversed(far_first(self.axis)):
                self.copy(distance, peer(self.axis, distance)).wait_recv()

        def drain(self):
            for distance in far_first(self.axis):
                self.copy(distance, place[self.axis]).wait_send()

    gram_lon = Stage(0, "lon", lambda index: gram_ref.at[index], gram_lon_ref)
    gram_lat = Stage(1, "lat", lambda index: gram_lat_ref.at[lat], gram_lat_ref)
    gram_tm = Stage(2, "tm", lambda index: gram_tm_ref.at[tm], gram_tm_ref)
    gram_all = Stage(3, "lon", lambda index: gram_all_ref.at[lon], gram_all_ref)
    shares_tm = Stage(4, "tm", lambda index: shares_ref.at[index], shares_tm_ref)
    shares_lat = Stage(5, "lat", lambda index: shares_lat_ref.at[lat], shares_lat_ref)
    shares_lon = Stage(6, "lon", lambda index: shares_lon_ref.at[lon], shares_lon_ref)

    loads[1].wait()
    loads[2].wait()
    pl.semaphore_wait(barrier, tm_count + lat_count + lon_count - 3)

    for part in range(CHUNKS):
        for distance in order:
            send_cells(part, distance, peer("tm", distance), tm).start()
        if part == 0:
            for distance in order:
                send_start(distance, peer("tm", distance), tm).start()

    own = [
        pltpu.make_async_copy(slab_ref.at[:, cells_of(tm, part)], cells_ref.at[part, hours_of(tm)], local_sem.at[part + 3])
        for part in range(CHUNKS)
    ]
    own_start = pltpu.make_async_copy(start_ref, starts_ref.at[hours_of(tm)], local_sem.at[CHUNKS + 3])
    for copy in own:
        copy.start()
    own_start.start()
    loads[0].wait()

    high_ref[...] = jnp.zeros_like(high_ref)
    low_ref[...] = jnp.zeros_like(low_ref)
    block_count = hours_all // BLOCK
    for lag, values in enumerate(toeplitz_blocks(sections_ref, block_count)):
        top = values.astype(jnp.bfloat16)
        rest = (values - top.astype(jnp.float32)).astype(jnp.bfloat16)
        for column in range(block_count - lag):
            where = (pl.ds((column + lag) * BLOCK, BLOCK), pl.ds(column * BLOCK, BLOCK))
            high_ref[where] = top
            low_ref[where] = rest

    own_start.wait()
    for distance in order:
        send_start(distance, peer("tm", distance), peer("tm", distance)).wait_recv()
    starts = starts_ref[...]

    gram_total = jnp.zeros((2 * width, 2 * width), jnp.float32)
    shares_total = jnp.zeros((hours_all, 2 * width), jnp.float32)
    half = hours_all // 2
    for part in range(CHUNKS):
        own[part].wait()
        for distance in order:
            send_cells(part, distance, peer("tm", distance), peer("tm", distance)).wait_recv()
        upper = [
            jnp.dot(ref[:half, :half], cells_ref[part, :half], preferred_element_type=jnp.float32)
            for ref in (high_ref, low_ref)
        ]
        lower = [
            jnp.dot(ref[half:], cells_ref[part], preferred_element_type=jnp.float32) for ref in (high_ref, low_ref)
        ]
        filtered = jnp.concatenate([upper[0] + upper[1], lower[0] + lower[1]], axis=0).astype(jnp.bfloat16)
        patterns = lax.dot_general(starts, filtered, (((0,), (0,)), ((), ())), preferred_element_type=jnp.float32)
        patterns_ref[:, part * chunk : (part + 1) * chunk] = patterns
        top = patterns.astype(jnp.bfloat16)
        rest = (patterns - top.astype(jnp.float32)).astype(jnp.bfloat16)
        both = jnp.concatenate([top, rest], axis=0)
        by_rows = (((1,), (1,)), ((), ()))
        gram_total = gram_total + lax.dot_general(both, both, by_rows, preferred_element_type=jnp.float32)
        shares_total = shares_total + lax.dot_general(filtered, both, by_rows, preferred_element_type=jnp.float32)

    def folded(value):
        return value + pltpu.roll(value, width, 1)

    gram_here = folded(gram_total[:width] + gram_total[width:])
    rows_each = width // lon_count
    for index in range(lon_count):
        gram_ref[index] = gram_here[index * rows_each : (index + 1) * rows_each]
    gram_lon.start()

    shares_here = folded(shares_total)
    left = lane_rows((hour_count // 2, 2 * width), 1) < width
    for index in range(tm_count):
        base = index * hour_count
        middle = base + hour_count // 2
        shares_ref[index] = jnp.where(left, shares_here[base:middle], shares_here[middle : base + hour_count])
    shares_tm.start()
    gram_lon_ref[lon] = gram_ref[lon]
    shares_tm_ref[tm] = shares_ref[tm]

    gram_lon.receive()
    gram_lat_ref[lat] = jnp.sum(gram_lon_ref[...], axis=0)
    gram_lat.start()
    gram_lat.receive()
    gram_tm_ref[tm] = jnp.sum(gram_lat_ref[...], axis=0)
    gram_tm.start()

    shares_tm.receive()
    shares_lat_ref[lat] = jnp.sum(shares_tm_ref[...], axis=0)
    shares_lat.start()

    gram_tm.receive()
    gram_all_ref[lon] = jnp.sum(gram_tm_ref[...], axis=0)
    gram_all.start()

    shares_lat.receive()
    shares_lon_ref[lon] = jnp.sum(shares_lat_ref[...], axis=0)
    shares_lon.start()

    gram_all.receive()
    gram = gram_all_ref[...].reshape(width, 2 * width)
    shape = (width, 2 * width)
    unit = jnp.where(lane_rows(shape, 1) - width == lane_rows(shape, 0), 1.0, 0.0)
    inverse = factor_inverse(jnp.where(lane_rows(shape, 1) < width, gram, unit))[:, :width]

    scaled = inverse * math.sqrt(cells_all)
    ortho = jnp.dot(scaled, patterns_ref[...], preferred_element_type=jnp.float32, precision=FULL)
    for group in range(own_cells // LANES):
        basis_ref[group] = ortho[:, group * LANES : (group + 1) * LANES]

    shares_lon.receive()
    packed = jnp.sum(shares_lon_ref[...], axis=0)
    shares = jnp.concatenate([packed, pltpu.roll(packed, width, 1)], axis=0)[:, :width]
    pcs_ref[...] = lax.dot_general(
        shares, inverse * math.sqrt(hours_all / cells_all), (((1,), (1,)), ((), ())),
        preferred_element_type=jnp.float32, precision=FULL,
    )

    for distance in order:
        for part in range(CHUNKS):
            send_cells(part, distance, peer("tm", distance), tm).wait_send()
        send_start(distance, peer("tm", distance), tm).wait_send()
    for stage in (gram_lon, gram_lat, gram_tm, gram_all, shares_tm, shares_lat, shares_lon):
        stage.drain()


def solution(mesh):
    tm_count, lat_count, lon_count = mesh.shape["tm"], mesh.shape["lat"], mesh.shape["lon"]

    def local(slab, start, sections):
        hour_count, cell_count = slab.shape
        width = start.shape[1]
        own_cells = cell_count // tm_count
        hours_all = hour_count * tm_count
        chunk = own_cells // CHUNKS
        rows_each = width // lon_count
        sizes = (tm_count, lat_count, lon_count, hour_count, width, own_cells)
        dma = pltpu.SemaphoreType.DMA
        f32, bf16 = jnp.float32, jnp.bfloat16
        return pl.pallas_call(
            functools.partial(kernel, sizes),
            out_shape=(
                jax.ShapeDtypeStruct((own_cells // LANES, width, LANES), f32),
                jax.ShapeDtypeStruct((hour_count, width), f32),
            ),
            in_specs=[pl.BlockSpec(memory_space=pltpu.HBM)] * 3,
            out_specs=(pl.BlockSpec(memory_space=pltpu.VMEM), pl.BlockSpec(memory_space=pltpu.VMEM)),
            scratch_shapes=[
                pltpu.VMEM((hour_count, cell_count), bf16),
                pltpu.VMEM((hour_count, width), bf16),
                pltpu.SMEM(sections.shape[::-1], f32),
                pltpu.VMEM((CHUNKS, hours_all, chunk), bf16),
                pltpu.VMEM((hours_all, width), bf16),
                pltpu.VMEM((hours_all, hours_all), bf16),
                pltpu.VMEM((hours_all, hours_all), bf16),
                pltpu.VMEM((width, own_cells), f32),
                pltpu.VMEM((lon_count, rows_each, 2 * width), f32),
                pltpu.VMEM((lon_count, rows_each, 2 * width), f32),
                pltpu.VMEM((lat_count, rows_each, 2 * width), f32),
                pltpu.VMEM((tm_count, rows_each, 2 * width), f32),
                pltpu.VMEM((lon_count, rows_each, 2 * width), f32),
                pltpu.VMEM((tm_count, hour_count // 2, 2 * width), f32),
                pltpu.VMEM((tm_count, hour_count // 2, 2 * width), f32),
                pltpu.VMEM((lat_count, hour_count // 2, 2 * width), f32),
                pltpu.VMEM((lon_count, hour_count // 2, 2 * width), f32),
                dma((CHUNKS + 4,)),
                dma((CHUNKS, tm_count)), dma((CHUNKS, tm_count)),
                dma((tm_count,)), dma((tm_count,)),
            ]
            + [
                dma((count,))
                for count in (lon_count, lat_count, tm_count, lon_count, tm_count, lat_count, lon_count)
                for _ in range(2)
            ],
            compiler_params=pltpu.CompilerParams(
                collective_id=0, has_side_effects=True, vmem_limit_bytes=67043328
            ),
        )(slab, start, sections.T)

    return jax.shard_map(
        local,
        mesh=mesh,
        in_specs=(P("tm", ("lat", "lon")), P("tm", None), P()),
        out_specs=(P(("lat", "lon", "tm"), None, None), P("tm", None)),
        check_vma=False,
    )
```
